512 devices in a mesh: tok: 64 (over y_lo, z, core), head: 8 (over y_hi, x).
Axes of the slice: x: 4, y: 4 (y_hi: 2, y_lo: 2; y = y_hi * 2 + y_lo), z: 16, core: 2. Of those that a mesh axis runs over, the one named last changes fastest.
Arguments:
- tokens: bfloat16 [8192, 3072], P('tok', 'head'), may hold values from -6 to 6
- norm_gain: bfloat16 [3072], replicated, may hold values from 0.099609375 to 1.8984375
- w_query: bfloat16 [3072, 3072], P('tok', 'head'), may hold values from -0.3125 to 0.3125
- w_key: bfloat16 [3072, 1024], P('tok', 'head'), may hold values from -0.3125 to 0.3125
- w_value: bfloat16 [3072, 1024], P('tok', 'head'), may hold values from -0.3125 to 0.3125
- w_out: bfloat16 [3072, 3072], P('tok', 'head'), may hold values from -0.109375 to 0.109375
- cache_keys: bfloat16 [64, 512, 1024], P(None, 'tok', 'head')
- cache_values: bfloat16 [64, 512, 1024], P(None, 'tok', 'head'), may hold values from -18 to 18
- lengths: int32 [64], P('tok'), may hold values from 2 to 512, as said below
- page_table: int32 [64, 32], P('tok'), may hold values from 0 to 31, each once within a row
Outputs:
- mixed: bfloat16 [8192, 3072], P('tok', 'head')
- decode_keys: bfloat16 [2048, 16, 1024], P('tok', None, 'head')
- decode_values: bfloat16 [2048, 16, 1024], P('tok', None, 'head')
The draws below stay inside these ranges and needn't reach their ends.
Inputs may be any that keep to these rules, and one draw needn't show every extreme that they name: lengths are 2 or more, and some request has exactly 512. Each row of page_table names every page slot once.
All inputs are finite; a program needn't handle non-finite values.
Results may differ from the reference program's by a relative error of at most 0.018.
Values may be sent and summed in bfloat16 or wider, within the bound.
A program may use at most 64 MiB of HBM per device.

```python
import math
import jax
import jax.numpy as jnp
from jax import lax

D = 3072
HQ = 24
KVH = 8
HD = 128
SPAN = 128
LMAX = 512
PAGE = 16
GROUP = 3
REQ = 64
NPAGE = 32
TOKENS = 8192
N_HEAD = 8


def draw_cache_keys(key, part):
    entries = jax.random.normal(jax.random.fold_in(key, 11), (REQ, LMAX, KVH * HD), jnp.float32)
    return (1.5 * entries).astype(jnp.bfloat16)


def draw_lengths(key, part):
    drawn = jax.random.randint(jax.random.fold_in(key, 21), (REQ,), 2, LMAX + 1)
    longest = jax.random.randint(jax.random.fold_in(key, 22), (), 0, REQ)
    return jnp.where(jnp.arange(REQ) == longest, LMAX, drawn).astype(jnp.int32)


def strengthened(entries, stream_key, source, target, shards_of, factor):
    def block_of(position):
        return (jnp.arange(entries.shape[position]) // (entries.shape[position] // shards_of)).reshape((-1,) + (1,) * (entries.ndim - 1 - position))

    near = jax.random.permutation(stream_key, shards_of)[block_of(target)]
    other_side = (block_of(target) + shards_of // 2) % shards_of
    return jnp.where((block_of(source) == near) | (block_of(source) == other_side), factor * entries, entries)


def shard_levels(own_key, shape, pieces, least, largest):
    factor_of = 1.0
    for dim, shards_of in pieces:
        heights = jax.random.uniform(jax.random.fold_in(jax.random.fold_in(own_key, 6), dim), (shards_of,), jnp.float32, least / len(pieces), largest / len(pieces))
        factor_of = factor_of * jnp.repeat(jnp.exp(heights), shape[dim] // shards_of).reshape((-1,) + (1,) * (len(shape) - 1 - dim))
    return factor_of


def bell_draw(rng, dims, scale, bound, shards=(), held_as=jnp.bfloat16):
    entries = scale * jax.random.normal(rng, dims, jnp.float32)
    if shards:
        entries = entries * shard_levels(rng, dims, shards, -0.22, 0.18)
    return jnp.clip(entries, -bound, bound).astype(held_as)


def bell_draw_with(own_key, extent, width, bound, cuts, heavy, kind=jnp.bfloat16):
    values = width * jax.random.normal(own_key, extent, jnp.float32)
    if cuts:
        values = values * shard_levels(own_key, extent, cuts, -0.22, 0.18)
    return jnp.clip(strengthened(values, jax.random.fold_in(own_key, 3), *heavy), -bound, bound).astype(kind)


def setup_inputs(seed: int = 0) -> dict:
    arg_keys = jax.random.split(jax.random.key(seed), 11)
    return {
        "tokens": bell_draw(arg_keys[0], (TOKENS, D), 1.0, 6.0, ((0, 64), (1, 8))),
        "norm_gain": jnp.clip(1.0 + 0.18 * jax.random.normal(arg_keys[1], (D,), jnp.float32), 0.099609375, 1.8984375).astype(jnp.bfloat16),
        "w_query": bell_draw_with(arg_keys[2], (D, HQ * HD), D ** -0.5, 0.3125, ((0, 64), (1, 8)), (0, 1, 64, 4.0)),
        "w_key": bell_draw_with(arg_keys[3], (D, KVH * HD), D ** -0.5, 0.3125, ((0, 64), (1, 8)), (0, 1, 64, 4.0)),
        "w_value": bell_draw_with(arg_keys[4], (D, KVH * HD), D ** -0.5, 0.3125, ((0, 64), (1, 8)), (0, 1, 64, 4.0)),
        "w_out": bell_draw(arg_keys[5], (D, HQ * HD), (HQ * HD) ** -0.5, 0.109375, ((0, 64), (1, 8))),
        "cache_keys": draw_cache_keys(jax.random.fold_in(arg_keys[10], 71), 0),
        "cache_values": bell_draw(arg_keys[7], (REQ, LMAX, KVH * HD), 3.0, 18.0, ((1, 64), (2, 8))),
        "lengths": draw_lengths(jax.random.fold_in(arg_keys[10], 71), 0),
        "page_table": jax.vmap(lambda own: jax.random.permutation(own, NPAGE))(jax.random.split(arg_keys[9], REQ)).reshape((REQ, NPAGE)).astype(jnp.int32),
    }


rope_base = 500000.0
norm_eps = 1e-05

def rotate(values, positions, head_size):
    row_count = values.shape[0]
    shaped = values.reshape(row_count, -1, head_size)
    half_size = head_size // 2
    exponent = jnp.arange(half_size, dtype=jnp.float32) * (2.0 / head_size)
    frequency = jnp.exp(-math.log(rope_base) * exponent)
    angles = positions.astype(jnp.float32)[:, None] * frequency[None, :]
    cosine = jnp.cos(angles)[:, None, :]
    sine_part = jnp.sin(angles)[:, None, :]
    first_half = shaped[:, :, :half_size]
    second_half = shaped[:, :, half_size:]
    turned = jnp.concatenate([first_half * cosine - second_half * sine_part, second_half * cosine + first_half * sine_part], axis=2)
    return turned.reshape(row_count, -1)

def attend_head(queries, cached_keys, cached_values, span_keys, span_values, live_slots, causal):
    score_scale = 1.0 / math.sqrt(queries.shape[1])
    numbers = (((1,), (1,)), ((), ()))
    cached_scores = lax.dot_general(queries, cached_keys, numbers, preferred_element_type=jnp.float32) * score_scale
    span_scores = lax.dot_general(queries, span_keys, numbers, preferred_element_type=jnp.float32) * score_scale
    cached_scores = jnp.where(live_slots[None, :], cached_scores, -jnp.inf)
    span_scores = jnp.where(causal, span_scores, -jnp.inf)
    row_max = jnp.maximum(lax.optimization_barrier(jnp.max(cached_scores, axis=1)), lax.optimization_barrier(jnp.max(span_scores, axis=1)))[:, None]
    cached_exp = jnp.exp(cached_scores - row_max)
    span_exp = jnp.exp(span_scores - row_max)
    row_total = lax.optimization_barrier(jnp.sum(cached_exp, axis=1, keepdims=True)) + lax.optimization_barrier(jnp.sum(span_exp, axis=1, keepdims=True))
    cached_weights = (cached_exp / row_total).astype(jnp.bfloat16)
    span_weights = (span_exp / row_total).astype(jnp.bfloat16)
    head_out = jnp.dot(cached_weights, cached_values, preferred_element_type=jnp.float32)
    head_out = head_out + jnp.dot(span_weights, span_values, preferred_element_type=jnp.float32)
    return head_out.astype(jnp.bfloat16)

def reference(tokens, norm_gain, w_query, w_key, w_value, w_out, cache_keys, cache_values, lengths, page_table):
    as_float = tokens.astype(jnp.float32)
    mean_square = lax.optimization_barrier(jnp.mean(as_float * as_float, axis=1, keepdims=True))
    normed = (as_float * lax.rsqrt(mean_square + norm_eps) * norm_gain.astype(jnp.float32)[None, :]).astype(jnp.bfloat16)
    positions = (jnp.repeat(lengths, SPAN) + jnp.tile(jnp.arange(SPAN, dtype=jnp.int32), REQ)).astype(jnp.int32)
    query_all = rotate(jnp.dot(normed, w_query, preferred_element_type=jnp.float32), positions, HD).astype(jnp.bfloat16)
    key_all = rotate(jnp.dot(normed, w_key, preferred_element_type=jnp.float32), positions, HD).astype(jnp.bfloat16)
    value_all = jnp.dot(normed, w_value, preferred_element_type=jnp.float32).astype(jnp.bfloat16)
    slot_ids = jnp.arange(LMAX, dtype=jnp.int32)
    live = slot_ids[None, :] < lengths[:, None]
    keys_live = jnp.where(live[:, :, None], cache_keys, jnp.zeros_like(cache_keys))
    values_live = jnp.where(live[:, :, None], cache_values, jnp.zeros_like(cache_values))
    request_ids = jnp.arange(REQ, dtype=jnp.int32)[:, None]
    page_keys = keys_live.reshape(REQ, NPAGE, PAGE, KVH * HD)
    page_values = values_live.reshape(REQ, NPAGE, PAGE, KVH * HD)
    decode_keys = jnp.zeros_like(page_keys).at[request_ids, page_table].set(page_keys).reshape(REQ * NPAGE, PAGE, KVH * HD)
    decode_values = jnp.zeros_like(page_values).at[request_ids, page_table].set(page_values).reshape(REQ * NPAGE, PAGE, KVH * HD)
    token_ids = jnp.arange(SPAN, dtype=jnp.int32)
    causal = token_ids[None, :] <= token_ids[:, None]

    def one_request(request):
        first_row = (request * SPAN).astype(jnp.int32)
        query_block = lax.dynamic_slice_in_dim(query_all, first_row, SPAN, 0)
        key_block = lax.dynamic_slice_in_dim(key_all, first_row, SPAN, 0)
        value_block = lax.dynamic_slice_in_dim(value_all, first_row, SPAN, 0)
        cached_k = keys_live[request]
        cached_v = values_live[request]
        live_slots = live[request]

        def one_head(head_number):
            group_start = (head_number // GROUP * HD).astype(jnp.int32)
            head_start = (head_number * HD).astype(jnp.int32)
            return attend_head(lax.dynamic_slice_in_dim(query_block, head_start, HD, 1), lax.dynamic_slice_in_dim(cached_k, group_start, HD, 1), lax.dynamic_slice_in_dim(cached_v, group_start, HD, 1), lax.dynamic_slice_in_dim(key_block, group_start, HD, 1), lax.dynamic_slice_in_dim(value_block, group_start, HD, 1), live_slots, causal)
        heads_out = lax.map(one_head, jnp.arange(HQ, dtype=jnp.int32))
        return jnp.transpose(heads_out, (1, 0, 2)).reshape(SPAN, HQ * HD)
    attention = lax.map(one_request, jnp.arange(REQ, dtype=jnp.int32)).reshape(TOKENS, HQ * HD)
    group_width = HQ * HD // N_HEAD
    summed = jnp.zeros((TOKENS, D), jnp.float32)
    for group in range(N_HEAD):
        columns = attention[:, group * group_width:(group + 1) * group_width]
        weight_cols = w_out[:, group * group_width:(group + 1) * group_width]
        partial_rounded = lax.dot_general(columns, weight_cols, (((1,), (1,)), ((), ())), preferred_element_type=jnp.float32).astype(jnp.bfloat16)
        partial_rounded = lax.optimization_barrier(partial_rounded)
        summed = summed + partial_rounded.astype(jnp.float32)
    mixed = summed.astype(jnp.bfloat16)
    return (mixed, decode_keys, decode_values)
```

```python
import functools
import math

import jax
import jax.numpy as jnp
from jax import lax
from jax.experimental import pallas as pl
from jax.experimental.pallas import tpu as pltpu
from jax.sharding import PartitionSpec as P

MESH = pl.DeviceIdType.MESH
HD = 128
NZ = 16
rope_base = 500000.0
norm_eps = 1e-05
NT = (((1,), (1,)), ((), ()))


def kernel(
    n_tok, n_head,
    len_ref, inv_ref, gain_ref, tok_in, wq_in, wk_in, wv_in, wo_in, ck_in, cv_in,
    mixed_ref, dk_ref, dv_ref,
    buf_t, buf_q, buf_kv, buf_o, buf_ck, buf_cv, normed, live_k, live_v, part_send, part_recv,
    own_sem, t_recv, q_recv, kv_recv, o_recv, c_recv, p_recv,
    t_send, w_send, c_send, p_send,
):
    me_t = lax.axis_index("tok")
    me_h = lax.axis_index("head")
    yl = me_t // (2 * NZ)
    z = lax.rem(me_t // 2, NZ)
    core = lax.rem(me_t, 2)
    yl_other = 1 - yl

    def tok_id(y, zz, c):
        return y * (2 * NZ) + lax.rem(zz + NZ, NZ) * 2 + c

    right = tok_id(yl, z + 1, core)
    left = tok_id(yl, z - 1, core)
    across = tok_id(yl_other, z, core)
    twin = tok_id(yl, z, 1 - core)

    own = [
        pltpu.make_async_copy(tok_in, buf_t.at[me_h], own_sem.at[0]),
        pltpu.make_async_copy(wq_in, buf_q.at[me_t], own_sem.at[1]),
        pltpu.make_async_copy(wk_in, buf_kv.at[me_t, :, pl.ds(0, HD)], own_sem.at[2]),
        pltpu.make_async_copy(wv_in, buf_kv.at[me_t, :, pl.ds(HD, HD)], own_sem.at[3]),
        pltpu.make_async_copy(wo_in, buf_o.at[me_t], own_sem.at[4]),
        pltpu.make_async_copy(ck_in.at[me_t], buf_ck.at[me_t], own_sem.at[5]),
        pltpu.make_async_copy(cv_in.at[me_t], buf_cv.at[me_t], own_sem.at[6]),
    ]
    for copy in own:
        copy.start()

    barrier = pltpu.get_barrier_semaphore()

    @pl.loop(1, n_tok)
    def _(i):
        pl.semaphore_signal(
            barrier, inc=1, device_id={"tok": lax.rem(me_t + i, n_tok)}, device_id_type=MESH
        )

    @pl.loop(1, n_head)
    def _(i):
        pl.semaphore_signal(
            barrier, inc=1, device_id={"head": lax.rem(me_h + i, n_head)}, device_id_type=MESH
        )

    for copy in own:
        copy.wait()
    pl.semaphore_wait(barrier, n_tok + n_head - 2)

    y_hi = me_h // 4
    x = lax.rem(me_h, 4)
    far_head = (1 - y_hi) * 4 + x

    def send_tokens(slot, target):
        pltpu.make_async_remote_copy(
            src_ref=buf_t.at[slot], dst_ref=buf_t.at[slot], send_sem=t_send,
            recv_sem=t_recv.at[slot], device_id={"head": target}, device_id_type=MESH,
        ).start()

    send_tokens(me_h, far_head)
    for i in (1, 3, 2):
        send_tokens(me_h, y_hi * 4 + lax.rem(x + i, 4))

    streams = {
        "q": (buf_q, q_recv, w_send.at[0], "zy"),
        "kv": (buf_kv, kv_recv, w_send.at[1], "yz"),
        "o": (buf_o, o_recv, w_send.at[2], "zy"),
    }

    def send(name, slot, target):
        buf, recv, sem, _ = streams[name]
        pltpu.make_async_remote_copy(
            src_ref=buf.at[slot], dst_ref=buf.at[slot], send_sem=sem,
            recv_sem=recv.at[slot], device_id={"tok": target}, device_id_type=MESH,
        ).start()

    def arrived(name, slot):
        buf, recv, _, _ = streams[name]
        pltpu.make_async_copy(buf.at[slot], buf.at[slot], recv.at[slot]).wait()

    def send_cache(first, last):
        @pl.loop(first, last)
        def _(i):
            peer = lax.rem(me_t + i, n_tok)
            for number, (source, target) in enumerate(((ck_in, buf_ck), (cv_in, buf_cv))):
                pltpu.make_async_remote_copy(
                    src_ref=source.at[peer], dst_ref=target.at[me_t], send_sem=c_send.at[number],
                    recv_sem=c_recv.at[number], device_id={"tok": peer}, device_id_type=MESH,
                ).start()

    half = NZ // 2
    order = ("q", "kv", "o")

    def start_stream(name):
        mode = streams[name][3]
        send(name, me_t, across)
        send(name, me_t, right)
        send(name, me_t, left)
        send(name, me_t, twin)

    def second_start(name):
        if streams[name][3] == "yz":
            arrived(name, across)
            send(name, across, right)
            send(name, across, left)
            send(name, across, twin)

    def hop(name, step):
        mode = streams[name][3]
        rows = (yl,) if mode == "zy" else (yl, yl_other)
        for y in rows:
            slot = tok_id(y, z - step, core)
            arrived(name, slot)
            if step < half:
                send(name, slot, right)
            if mode == "zy":
                send(name, slot, across)
            send(name, slot, twin)
            if step < half:
                slot = tok_id(y, z + step, core)
                arrived(name, slot)
                if step < half - 1:
                    send(name, slot, left)
                if mode == "zy":
                    send(name, slot, across)
                send(name, slot, twin)

    def across_arrivals(name, step):
        if streams[name][3] != "zy":
            return
        slots = [tok_id(yl_other, z - step, core)]
        if 0 < step < half:
            slots.append(tok_id(yl_other, z + step, core))
        for slot in slots:
            arrived(name, slot)
            send(name, slot, twin)

    for name in order:
        start_stream(name)
    for name in order:
        second_start(name)
    send_cache(1, 8)
    for step in range(1, half + 1):
        for name in order:
            hop(name, step)
            across_arrivals(name, step - 1)
        if step == 1:
            pltpu.make_async_copy(buf_t.at[far_head], buf_t.at[far_head], t_recv.at[far_head]).wait()
            for i in (1, 3, 2):
                send_tokens(far_head, y_hi * 4 + lax.rem(x + i, 4))
        if step < half:
            send_cache(step * 8, step * 8 + 8)
    for name in order:
        across_arrivals(name, half)

    for i in range(1, 4):
        for y in range(2):
            slot = y * 4 + lax.rem(x + i, 4)
            pltpu.make_async_copy(buf_t.at[slot], buf_t.at[slot], t_recv.at[slot]).wait()
    rows = tok_in.shape[0]
    width = tok_in.shape[1]
    total = jnp.zeros((rows, 1), jnp.float32)
    for h in range(n_head):
        part = buf_t[h].astype(jnp.float32)
        total += jnp.sum(part * part, axis=1, keepdims=True)
    scale = lax.rsqrt(total / (n_head * width) + norm_eps)
    for h in range(n_head):
        gain = gain_ref[:, h * width:(h + 1) * width].astype(jnp.float32)
        normed[h] = (buf_t[h].astype(jnp.float32) * scale * gain).astype(jnp.bfloat16)

    length = len_ref[0]
    for number, (buf, live, out) in enumerate(((buf_ck, live_k, dk_ref), (buf_cv, live_v, dv_ref))):
        pltpu.make_async_copy(
            buf.at[pl.ds(0, n_tok - 1)], buf.at[pl.ds(0, n_tok - 1)], c_recv.at[number]
        ).wait()
        entries = buf[...].astype(jnp.float32)
        slots, head_size = entries.shape[0] * entries.shape[1], entries.shape[2]
        entries = entries.reshape(slots, head_size)
        slot_ids = lax.broadcasted_iota(jnp.int32, (slots, head_size), 0)
        entries = jnp.where(slot_ids < length, entries, 0.0)
        live[...] = entries.reshape(live.shape).astype(jnp.bfloat16)
        for page in range(out.shape[0]):
            out[page] = live[inv_ref[page]]

    for name in order:
        for y in range(2):
            for zz in range(NZ):
                arrived(name, tok_id(y, zz, 1 - core))

    group = n_tok // n_head
    depth = buf_q.shape[1]
    q_sum = jnp.zeros((rows, buf_q.shape[2]), jnp.float32)
    kv_sum = jnp.zeros((rows, buf_kv.shape[2]), jnp.float32)
    for h in range(n_head):
        lhs = normed[h]
        wq = buf_q[pl.ds(h * group, group)].reshape(group * depth, buf_q.shape[2])
        wkv = buf_kv[pl.ds(h * group, group)].reshape(group * depth, buf_kv.shape[2])
        q_sum += jnp.dot(lhs, wq, preferred_element_type=jnp.float32)
        kv_sum += jnp.dot(lhs, wkv, preferred_element_type=jnp.float32)

    lane = lax.broadcasted_iota(jnp.int32, (rows, HD), 1)
    row = lax.broadcasted_iota(jnp.int32, (rows, HD), 0)
    exponent = lax.rem(lane, HD // 2).astype(jnp.float32) * (2.0 / HD)
    frequency = jnp.exp(-math.log(rope_base) * exponent)
    angles = (row + length).astype(jnp.float32) * frequency
    cosine = jnp.cos(angles)
    sine = jnp.sin(angles)
    sine = jnp.where(lane < HD // 2, -sine, sine)

    def rope(v):
        return (v * cosine + pltpu.roll(v, HD // 2, 1) * sine).astype(jnp.bfloat16)

    key_new = rope(kv_sum[:, :HD])
    value_new = kv_sum[:, HD:].astype(jnp.bfloat16)
    keys = live_k[...].reshape(n_tok * buf_ck.shape[1], HD)
    values = live_v[...].reshape(n_tok * buf_ck.shape[1], HD)
    score_scale = 1.0 / math.sqrt(HD)
    cached_ids = lax.broadcasted_iota(jnp.int32, (rows, keys.shape[0]), 1)
    causal = lax.broadcasted_iota(jnp.int32, (rows, rows), 1) <= lax.broadcasted_iota(
        jnp.int32, (rows, rows), 0
    )
    heads_out = []
    for head in range(q_sum.shape[1] // HD):
        query = rope(q_sum[:, head * HD:(head + 1) * HD])
        cached = lax.dot_general(query, keys, NT, preferred_element_type=jnp.float32) * score_scale
        span = lax.dot_general(query, key_new, NT, preferred_element_type=jnp.float32) * score_scale
        cached = jnp.where(cached_ids < length, cached, -jnp.inf)
        span = jnp.where(causal, span, -jnp.inf)
        top = jnp.maximum(
            jnp.max(cached, axis=1, keepdims=True), jnp.max(span, axis=1, keepdims=True)
        )
        cached = jnp.exp(cached - top)
        span = jnp.exp(span - top)
        whole = jnp.sum(cached, axis=1, keepdims=True) + jnp.sum(span, axis=1, keepdims=True)
        out = jnp.dot((cached / whole).astype(jnp.bfloat16), values, preferred_element_type=jnp.float32)
        out += jnp.dot((span / whole).astype(jnp.bfloat16), value_new, preferred_element_type=jnp.float32)
        heads_out.append(out.astype(jnp.bfloat16))
    attention = jnp.concatenate(heads_out, axis=1)

    def partial_block(g):
        block = buf_o[pl.ds(g * group, group)].reshape(group * depth, buf_o.shape[2])
        return lax.dot_general(
            attention, block, NT, preferred_element_type=jnp.float32
        ).astype(jnp.bfloat16)

    def part_copy(i):
        return pltpu.make_async_remote_copy(
            src_ref=part_send.at[i - 1], dst_ref=part_recv.at[i - 1], send_sem=p_send.at[i - 1],
            recv_sem=p_recv.at[i - 1], device_id={"head": lax.rem(me_h + i, n_head)},
            device_id_type=MESH,
        )

    offsets = (4, 6, 2, 5, 3, 7, 1)
    for i in offsets:
        part_send[i - 1] = partial_block(lax.rem(me_h + i, n_head))
        part_copy(i).start()
    mixed = partial_block(me_h).astype(jnp.float32)
    for i in offsets[::-1]:
        part_copy(i).wait_recv()
        mixed += part_recv[i - 1].astype(jnp.float32)
    mixed_ref[...] = mixed.astype(jnp.bfloat16)

    for i in offsets:
        part_copy(i).wait_send()
    pltpu.make_async_copy(
        buf_t.at[pl.ds(0, n_head - 1)], buf_t.at[pl.ds(0, n_head - 1)], t_send
    ).wait()
    for number, buf in enumerate((buf_ck, buf_cv)):
        pltpu.make_async_copy(
            buf.at[pl.ds(0, n_tok - 1)], buf.at[pl.ds(0, n_tok - 1)], c_send.at[number]
        ).wait()
    for name in order:
        buf, _, sem, _ = streams[name]
        pltpu.make_async_copy(
            buf.at[pl.ds(0, n_tok - 1)], buf.at[pl.ds(0, n_tok - 1)], sem
        ).wait()


def solution(mesh):
    n_tok, n_head = mesh.shape["tok"], mesh.shape["head"]

    def shards(tokens, gain, w_query, w_key, w_value, w_out, cache_keys, cache_values, lengths, page_table):
        rows, width = tokens.shape
        pages = page_table.shape[1]
        depth, head_cols = w_query.shape
        page_ids = jnp.arange(pages, dtype=jnp.int32)
        inverse = jnp.sum(
            jnp.where(page_table[0][:, None] == page_ids[None, :], page_ids[:, None], 0), axis=0
        ).astype(jnp.int32)
        page_size = n_tok * cache_keys.shape[1] // pages
        paged = (pages, page_size, cache_keys.shape[2])
        bf16 = jnp.bfloat16
        dma = pltpu.SemaphoreType.DMA
        hbm = pl.BlockSpec(memory_space=pl.ANY)
        vmem = pl.BlockSpec(memory_space=pltpu.VMEM)
        smem = pl.BlockSpec(memory_space=pltpu.SMEM)
        return pl.pallas_call(
            functools.partial(kernel, n_tok, n_head),
            out_shape=(
                jax.ShapeDtypeStruct((rows, width), bf16),
                jax.ShapeDtypeStruct(paged, bf16),
                jax.ShapeDtypeStruct(paged, bf16),
            ),
            in_specs=[smem, smem, vmem] + [hbm] * 7,
            out_specs=(vmem, vmem, vmem),
            scratch_shapes=[
                pltpu.VMEM((n_head, rows, width), bf16),
                pltpu.VMEM((n_tok, depth, head_cols), bf16),
                pltpu.VMEM((n_tok, depth, 2 * HD), bf16),
                pltpu.VMEM((n_tok, depth, head_cols), bf16),
                pltpu.VMEM((n_tok,) + cache_keys.shape[1:], bf16),
                pltpu.VMEM((n_tok,) + cache_keys.shape[1:], bf16),
                pltpu.VMEM((n_head, rows, width), bf16),
                pltpu.VMEM(paged, bf16),
                pltpu.VMEM(paged, bf16),
                pltpu.VMEM((n_head - 1, rows, width), bf16),
                pltpu.VMEM((n_head - 1, rows, width), bf16),
                dma((7,)),
                dma((n_head,)),
                dma((n_tok,)),
                dma((n_tok,)),
                dma((n_tok,)),
                dma((2,)),
                dma((n_head - 1,)),
                dma,
                dma((3,)),
                dma((2,)),
                dma((n_head - 1,)),
            ],
            compiler_params=pltpu.CompilerParams(collective_id=0, has_side_effects=True),
        )(lengths, inverse, gain[None, :], tokens, w_query, w_key, w_value, w_out, cache_keys, cache_values)

    in_specs = (
        P("tok", "head"), P(), P("tok", "head"), P("tok", "head"), P("tok", "head"),
        P("tok", "head"), P(None, "tok", "head"), P(None, "tok", "head"), P("tok"), P("tok", None),
    )
    out_specs = (P("tok", "head"), P("tok", None, "head"), P("tok", None, "head"))
    return jax.shard_map(shards, mesh=mesh, in_specs=in_specs, out_specs=out_specs, check_vma=False)
```

```python
import functools
import math

import jax
import jax.numpy as jnp
from jax import lax
from jax.experimental import pallas as pl
from jax.experimental.pallas import tpu as pltpu
from jax.sharding import PartitionSpec as P

MESH = pl.DeviceIdType.MESH
HD = 128
NZ = 16
LAG = 4
rope_base = 500000.0
norm_eps = 1e-05
NT = (((1,), (1,)), ((), ()))


def kernel(
    n_tok, n_head,
    len_ref, page_ref, gain_ref, tok_in, wq_in, wk_in, wv_in, wo_in, ck_in, cv_in,
    mixed_ref, dk_ref, dv_ref,
    buf_t, buf_q, buf_kv, buf_o, buf_ck, buf_cv, normed, live_k, live_v, part_send, part_recv,
    q_s, kv_s, cos_s, sin_s, att_s, inv_s,
    own_sem, t_recv, q_recv, kv_recv, o_recv, c_recv, p_recv,
    t_send, w_send, c_send, p_send,
):
    me_t = lax.axis_index("tok")
    me_h = lax.axis_index("head")
    yl = me_t // (2 * NZ)
    z = lax.rem(me_t // 2, NZ)
    core = lax.rem(me_t, 2)
    yl_other = 1 - yl
    y_hi = me_h // 4
    x = lax.rem(me_h, 4)
    y_far = 1 - y_hi
    far_head = y_far * 4 + x
    rows, width = tok_in.shape

    def tok_id(y, zz, c):
        return y * (2 * NZ) + lax.rem(zz + NZ, NZ) * 2 + c

    def head_id(y, i):
        return y * 4 + lax.rem(x + i, 4)

    right = tok_id(yl, z + 1, core)
    left = tok_id(yl, z - 1, core)
    across = tok_id(yl_other, z, core)
    twin = tok_id(yl, z, 1 - core)

    own = [
        pltpu.make_async_copy(wq_in, buf_q.at[me_t], own_sem.at[0]),
        pltpu.make_async_copy(wk_in, buf_kv.at[me_t, :, pl.ds(0, HD)], own_sem.at[1]),
        pltpu.make_async_copy(wv_in, buf_kv.at[me_t, :, pl.ds(HD, HD)], own_sem.at[2]),
        pltpu.make_async_copy(tok_in, buf_t.at[me_h], own_sem.at[3]),
        pltpu.make_async_copy(wo_in, buf_o.at[me_t], own_sem.at[4]),
        pltpu.make_async_copy(ck_in.at[me_t], buf_ck.at[me_t], own_sem.at[5]),
        pltpu.make_async_copy(cv_in.at[me_t], buf_cv.at[me_t], own_sem.at[6]),
    ]
    for copy in own:
        copy.start()

    barrier = pltpu.get_barrier_semaphore()
    for target in (right, left, across, twin):
        pl.semaphore_signal(barrier, inc=1, device_id={"tok": target}, device_id_type=MESH)
    for target in (head_id(y_hi, 1), head_id(y_hi, 2), head_id(y_hi, 3), far_head):
        pl.semaphore_signal(barrier, inc=1, device_id={"head": target}, device_id_type=MESH)

    length = len_ref[0]
    lane = lax.broadcasted_iota(jnp.int32, (rows, HD), 1)
    row = lax.broadcasted_iota(jnp.int32, (rows, HD), 0)
    exponent = lax.rem(lane, HD // 2).astype(jnp.float32) * (2.0 / HD)
    frequency = jnp.exp(-math.log(rope_base) * exponent)
    angles = (row + length).astype(jnp.float32) * frequency
    sine = jnp.sin(angles)
    cos_s[...] = jnp.cos(angles)
    sin_s[...] = jnp.where(lane < HD // 2, -sine, sine)

    for copy in own:
        copy.wait()
    pl.semaphore_wait(barrier, 8)

    def send_tokens(slot, target):
        pltpu.make_async_remote_copy(
            src_ref=buf_t.at[slot], dst_ref=buf_t.at[slot], send_sem=t_send,
            recv_sem=t_recv.at[slot], device_id={"head": target}, device_id_type=MESH,
        ).start()

    def tokens_arrived(slot):
        pltpu.make_async_copy(buf_t.at[slot], buf_t.at[slot], t_recv.at[slot]).wait()

    streams = {
        "q": (buf_q, q_recv, w_send.at[0], "zy"),
        "kv": (buf_kv, kv_recv, w_send.at[1], "yz"),
        "o": (buf_o, o_recv, w_send.at[2], "zy"),
    }

    def send(name, slot, target):
        buf, recv, sem, _ = streams[name]
        pltpu.make_async_remote_copy(
            src_ref=buf.at[slot], dst_ref=buf.at[slot], send_sem=sem,
            recv_sem=recv.at[slot], device_id={"tok": target}, device_id_type=MESH,
        ).start()

    def arrived(name, slot):
        buf, recv, _, _ = streams[name]
        pltpu.make_async_copy(buf.at[slot], buf.at[slot], recv.at[slot]).wait()

    def send_cache(peer):
        for number, (source, target) in enumerate(((ck_in, buf_ck), (cv_in, buf_cv))):
            pltpu.make_async_remote_copy(
                src_ref=source.at[peer], dst_ref=target.at[me_t], send_sem=c_send.at[number],
                recv_sem=c_recv.at[number], device_id={"tok": peer}, device_id_type=MESH,
            ).start()

    half = NZ // 2

    def at_step(y, step, c):
        if step == 0:
            return [tok_id(y, z, c)]
        slots = [tok_id(y, z - step, c)]
        return slots + [tok_id(y, z + step, c)] if step < half else slots

    def start_stream(name):
        send(name, me_t, across)
        send(name, me_t, right)
        send(name, me_t, left)
        send(name, me_t, twin)

    def second_start(name):
        arrived(name, across)
        send(name, across, right)
        send(name, across, left)
        send(name, across, twin)

    def hop(name, step):
        mode = streams[name][3]
        for y in (yl,) if mode == "zy" else (yl, yl_other):
            for number, slot in enumerate(at_step(y, step, core)):
                arrived(name, slot)
                if step < half - number:
                    send(name, slot, left if number else right)
                if mode == "zy":
                    send(name, slot, across)
                send(name, slot, twin)

    def across_arrivals(name, step):
        for slot in at_step(yl_other, step, core):
            arrived(name, slot)
            send(name, slot, twin)

    start_stream("q")
    start_stream("kv")
    send_tokens(me_h, far_head)
    for i in (1, 3, 2):
        send_tokens(me_h, head_id(y_hi, i))
    second_start("kv")
    send_cache(twin)

    @pl.loop(0, page_ref.shape[1])
    def _(slot):
        page = jnp.int32(0)
        for p in range(page_ref.shape[1]):
            page = jnp.where(page_ref[0, p] == slot, jnp.int32(p), page)
        inv_s[slot] = page

    def cache_step(step):
        if step <= half:
            for slot in at_step(yl, step, core):
                send_cache(slot)
        if 1 <= step <= half + 1:
            for slot in at_step(yl_other, step - 1, core):
                send_cache(slot)
            if step == 1:
                arrived("q", twin)
            if step >= 2:
                for slot in at_step(yl, step - 1, 1 - core):
                    arrived("q", slot)
                    send_cache(slot)
        if step >= 2:
            for slot in at_step(yl_other, step - 2, 1 - core):
                arrived("q", slot)
                send_cache(slot)

    def square_sum():
        for slot in [head_id(y_hi, i) for i in (1, 2, 3)] + [head_id(y_far, i) for i in (1, 2, 3)]:
            tokens_arrived(slot)
        total = jnp.zeros((rows, 1), jnp.float32)
        for h in range(n_head):
            part = buf_t[h].astype(jnp.float32)
            total += jnp.sum(part * part, axis=1, keepdims=True)
        return lax.rsqrt(total / (n_head * width) + norm_eps)

    def normalise(scale):
        for h in range(n_head):
            gain = gain_ref[pl.ds(h * width, width)].astype(jnp.float32)[None, :]
            normed[h] = (buf_t[h].astype(jnp.float32) * scale * gain).astype(jnp.bfloat16)

    group = n_tok // n_head
    depth = buf_q.shape[1]

    def project():
        for y in range(2):
            for zz in range(NZ):
                arrived("kv", tok_id(y, zz, 1 - core))
        q_sum = jnp.zeros(q_s.shape, jnp.float32)
        kv_sum = jnp.zeros(kv_s.shape, jnp.float32)
        for h in range(n_head):
            lhs = normed[h]
            wq = buf_q[pl.ds(h * group, group)].reshape(group * depth, buf_q.shape[2])
            wkv = buf_kv[pl.ds(h * group, group)].reshape(group * depth, buf_kv.shape[2])
            q_sum += jnp.dot(lhs, wq, preferred_element_type=jnp.float32)
            kv_sum += jnp.dot(lhs, wkv, preferred_element_type=jnp.float32)

        def rope(v):
            return (v * cos_s[...] + pltpu.roll(v, HD // 2, 1) * sin_s[...]).astype(jnp.bfloat16)

        for head in range(q_s.shape[1] // HD):
            q_s[:, head * HD:(head + 1) * HD] = rope(q_sum[:, head * HD:(head + 1) * HD])
        kv_s[:, :HD] = rope(kv_sum[:, :HD])
        kv_s[:, HD:] = kv_sum[:, HD:].astype(jnp.bfloat16)

    def page_caches():
        for number, (buf, live, out) in enumerate(((buf_ck, live_k, dk_ref), (buf_cv, live_v, dv_ref))):
            pltpu.make_async_copy(
                buf.at[pl.ds(0, n_tok - 1)], buf.at[pl.ds(0, n_tok - 1)], c_recv.at[number]
            ).wait()
            entries = buf[...].astype(jnp.float32)
            slots, head_size = entries.shape[0] * entries.shape[1], entries.shape[2]
            entries = entries.reshape(slots, head_size)
            slot_ids = lax.broadcasted_iota(jnp.int32, (slots, head_size), 0)
            entries = jnp.where(slot_ids < length, entries, 0.0)
            live[...] = entries.reshape(live.shape).astype(jnp.bfloat16)
            for page in range(out.shape[0]):
                out[page] = live[inv_s[page]]

    def attend(head):
        columns = slice(head * HD, (head + 1) * HD)
        keys = live_k[...].reshape(n_tok * buf_ck.shape[1], HD)
        values = live_v[...].reshape(n_tok * buf_ck.shape[1], HD)
        score_scale = 1.0 / math.sqrt(HD)
        cached_ids = lax.broadcasted_iota(jnp.int32, (rows, keys.shape[0]), 1)
        causal = lax.broadcasted_iota(jnp.int32, (rows, rows), 1) <= lax.broadcasted_iota(
            jnp.int32, (rows, rows), 0
        )
        query = q_s[:, columns]
        cached = lax.dot_general(query, keys, NT, preferred_element_type=jnp.float32) * score_scale
        span = lax.dot_general(query, kv_s[:, :HD], NT, preferred_element_type=jnp.float32) * score_scale
        cached = jnp.where(cached_ids < length, cached, -jnp.inf)
        span = jnp.where(causal, span, -jnp.inf)
        top = jnp.maximum(
            jnp.max(cached, axis=1, keepdims=True), jnp.max(span, axis=1, keepdims=True)
        )
        cached = jnp.exp(cached - top)
        span = jnp.exp(span - top)
        whole = jnp.sum(cached, axis=1, keepdims=True) + jnp.sum(span, axis=1, keepdims=True)
        out = jnp.dot((cached / whole).astype(jnp.bfloat16), values, preferred_element_type=jnp.float32)
        out += jnp.dot((span / whole).astype(jnp.bfloat16), kv_s[:, HD:], preferred_element_type=jnp.float32)
        att_s[:, columns] = out.astype(jnp.bfloat16)

    heads = q_s.shape[1] // HD
    scale = None
    for step in range(1, half + LAG + 1):
        if step <= half:
            hop("q", step)
            across_arrivals("q", step - 1)
            hop("kv", step)
        if step == half + 1:
            across_arrivals("q", half)
        if step == LAG:
            start_stream("o")
        if step > LAG:
            hop("o", step - LAG)
            across_arrivals("o", step - LAG - 1)
        if step <= half + 2:
            cache_step(step)
        if step == 1:
            tokens_arrived(far_head)
            for i in (1, 3, 2):
                send_tokens(far_head, head_id(y_hi, i))
        if step == half - 1:
            scale = square_sum()
            normalise(scale)
        if step == half + 2:
            project()
        if step == half + 3:
            page_caches()
            attend(0)
        if step == half + 4:
            for head in range(1, heads):
                attend(head)
    across_arrivals("o", half)
    for y in range(2):
        for zz in range(NZ):
            arrived("o", tok_id(y, zz, 1 - core))

    def partial_block(g):
        block = buf_o[pl.ds(g * group, group)].reshape(group * depth, buf_o.shape[2])
        return lax.dot_general(att_s[...], block, NT, preferred_element_type=jnp.float32)

    def part_copy(slot, target):
        return pltpu.make_async_remote_copy(
            src_ref=part_send.at[slot], dst_ref=part_recv.at[slot], send_sem=p_send.at[slot],
            recv_sem=p_recv.at[slot], device_id={"head": target}, device_id_type=MESH,
        )

    copies = [part_copy(i - 1, head_id(y_hi, i)) for i in (1, 2, 3)]
    copies += [part_copy(i + 2, head_id(y_hi, i)) for i in (1, 2, 3)]
    copies += [part_copy(6, far_head)]
    for i in (2, 1, 3):
        part_send[i - 1] = partial_block(head_id(y_far, i)).astype(jnp.bfloat16)
        copies[i - 1].start()
    far_sum = partial_block(far_head)
    for i in (2, 1, 3):
        part_send[i + 2] = partial_block(head_id(y_hi, i)).astype(jnp.bfloat16)
        copies[i + 2].start()
    for i in (1, 3, 2):
        copies[i - 1].wait_recv()
        far_sum += part_recv[i - 1].astype(jnp.float32)
    part_send[6] = far_sum.astype(jnp.bfloat16)
    copies[6].start()
    mixed = partial_block(me_h)
    for i in (1, 3, 2):
        copies[i + 2].wait_recv()
        mixed += part_recv[i + 2].astype(jnp.float32)
    copies[6].wait_recv()
    mixed_ref[...] = (mixed + part_recv[6].astype(jnp.float32)).astype(mixed_ref.dtype)

    for copy in copies:
        copy.wait_send()
    pltpu.make_async_copy(
        buf_t.at[pl.ds(0, n_head - 1)], buf_t.at[pl.ds(0, n_head - 1)], t_send
    ).wait()
    for number, buf in enumerate((buf_ck, buf_cv)):
        pltpu.make_async_copy(
            buf.at[pl.ds(0, n_tok - 1)], buf.at[pl.ds(0, n_tok - 1)], c_send.at[number]
        ).wait()
    for buf, _, sem, _ in streams.values():
        pltpu.make_async_copy(
            buf.at[pl.ds(0, n_tok - 1)], buf.at[pl.ds(0, n_tok - 1)], sem
        ).wait()


def solution(mesh):
    n_tok, n_head = mesh.shape["tok"], mesh.shape["head"]

    def shards(tokens, gain, w_query, w_key, w_value, w_out, cache_keys, cache_values, lengths, page_table):
        rows, width = tokens.shape
        pages = page_table.shape[1]
        depth, head_cols = w_query.shape
        page_size = n_tok * cache_keys.shape[1] // pages
        paged = (pages, page_size, cache_keys.shape[2])
        bf16 = jnp.bfloat16
        dma = pltpu.SemaphoreType.DMA
        hbm = pl.BlockSpec(memory_space=pl.ANY)
        vmem = pl.BlockSpec(memory_space=pltpu.VMEM)
        smem = pl.BlockSpec(memory_space=pltpu.SMEM)
        return pl.pallas_call(
            functools.partial(kernel, n_tok, n_head),
            out_shape=(
                jax.ShapeDtypeStruct((rows, width), bf16),
                jax.ShapeDtypeStruct(paged, bf16),
                jax.ShapeDtypeStruct(paged, bf16),
            ),
            in_specs=[smem, smem, vmem] + [hbm] * 7,
            out_specs=(vmem, vmem, vmem),
            scratch_shapes=[
                pltpu.VMEM((n_head, rows, width), bf16),
                pltpu.VMEM((n_tok, depth, head_cols), bf16),
                pltpu.VMEM((n_tok, depth, 2 * HD), bf16),
                pltpu.VMEM((n_tok, depth, head_cols), bf16),
                pltpu.VMEM((n_tok,) + cache_keys.shape[1:], bf16),
                pltpu.VMEM((n_tok,) + cache_keys.shape[1:], bf16),
                pltpu.VMEM((n_head, rows, width), bf16),
                pltpu.VMEM(paged, bf16),
                pltpu.VMEM(paged, bf16),
                pltpu.VMEM((n_head - 1, rows, width), bf16),
                pltpu.VMEM((n_head - 1, rows, width), bf16),
                pltpu.VMEM((rows, head_cols), bf16),
                pltpu.VMEM((rows, 2 * HD), bf16),
                pltpu.VMEM((rows, HD), jnp.float32),
                pltpu.VMEM((rows, HD), jnp.float32),
                pltpu.VMEM((rows, head_cols), bf16),
                pltpu.SMEM((pages,), jnp.int32),
                dma((7,)),
                dma((n_head,)),
                dma((n_tok,)),
                dma((n_tok,)),
                dma((n_tok,)),
                dma((2,)),
                dma((n_head - 1,)),
                dma,
                dma((3,)),
                dma((2,)),
                dma((n_head - 1,)),
            ],
            compiler_params=pltpu.CompilerParams(collective_id=0, has_side_effects=True),
        )(lengths, page_table, gain, tokens, w_query, w_key, w_value, w_out, cache_keys, cache_values)

    in_specs = (
        P("tok", "head"), P(), P("tok", "head"), P("tok", "head"), P("tok", "head"),
        P("tok", "head"), P(None, "tok", "head"), P(None, "tok", "head"), P("tok"), P("tok", None),
    )
    out_specs = (P("tok", "head"), P("tok", None, "head"), P("tok", None, "head"))
    return jax.shard_map(shards, mesh=mesh, in_specs=in_specs, out_specs=out_specs, check_vma=False)
```

```python
import functools
import math

import jax
import jax.numpy as jnp
from jax import lax
from jax.experimental import pallas as pl
from jax.experimental.pallas import tpu as pltpu
from jax.sharding import PartitionSpec as P

MESH = pl.DeviceIdType.MESH
HD = 128
NZ = 16
LAG = 1
GAP = 2
LAST = max(LAG, 3)
MODE_Q, MODE_KV, MODE_O = "zy", "yz", "zy"
rope_base = 500000.0
norm_eps = 1e-05
NT = (((1,), (1,)), ((), ()))


def kernel(
    n_tok, n_head,
    len_ref, page_ref, gain_ref, tok_in, wq_in, wk_in, wv_in, wo_in, ck_in, cv_in,
    mixed_ref, dk_ref, dv_ref,
    buf_t, buf_q, buf_kv, buf_o, buf_in, buf_c, normed, live_k, live_v, part_send, part_recv,
    q_s, kv_s, cos_s, sin_s, att_s, inv_s,
    own_sem, t_recv, q_recv, kv_recv, o_recv, c_recv, p_recv,
    t_send, w_send, c_send, p_send,
):
    me_t = lax.axis_index("tok")
    me_h = lax.axis_index("head")
    yl = me_t // (2 * NZ)
    z = lax.rem(me_t // 2, NZ)
    core = lax.rem(me_t, 2)
    yl_other = 1 - yl
    y_hi = me_h // 4
    x = lax.rem(me_h, 4)
    y_far = 1 - y_hi
    far_head = y_far * 4 + x
    rows, width = tok_in.shape

    def tok_id(y, zz, c):
        return y * (2 * NZ) + lax.rem(zz + NZ, NZ) * 2 + c

    def head_id(y, i):
        return y * 4 + lax.rem(x + i, 4)

    right = tok_id(yl, z + 1, core)
    left = tok_id(yl, z - 1, core)
    across = tok_id(yl_other, z, core)
    twin = tok_id(yl, z, 1 - core)

    own = [
        pltpu.make_async_copy(wq_in, buf_q.at[me_t], own_sem.at[0]),
        pltpu.make_async_copy(wk_in, buf_kv.at[me_t, :, pl.ds(0, HD)], own_sem.at[1]),
        pltpu.make_async_copy(wv_in, buf_kv.at[me_t, :, pl.ds(HD, HD)], own_sem.at[2]),
        pltpu.make_async_copy(tok_in, buf_t.at[me_h], own_sem.at[3]),
        pltpu.make_async_copy(wo_in, buf_o.at[me_t], own_sem.at[4]),
        pltpu.make_async_copy(ck_in, buf_in.at[:, 0], own_sem.at[5]),
        pltpu.make_async_copy(cv_in, buf_in.at[:, 1], own_sem.at[6]),
        pltpu.make_async_copy(ck_in.at[me_t], buf_c.at[me_t, 0], own_sem.at[7]),
        pltpu.make_async_copy(cv_in.at[me_t], buf_c.at[me_t, 1], own_sem.at[8]),
    ]
    for copy in own:
        copy.start()

    barrier = pltpu.get_barrier_semaphore()
    for target in (right, left, across, twin):
        pl.semaphore_signal(barrier, inc=1, device_id={"tok": target}, device_id_type=MESH)
    for target in (head_id(y_hi, 1), head_id(y_hi, 2), head_id(y_hi, 3), far_head):
        pl.semaphore_signal(barrier, inc=1, device_id={"head": target}, device_id_type=MESH)

    length = len_ref[0]
    lane = lax.broadcasted_iota(jnp.int32, (rows, HD), 1)
    row = lax.broadcasted_iota(jnp.int32, (rows, HD), 0)
    exponent = lax.rem(lane, HD // 2).astype(jnp.float32) * (2.0 / HD)
    frequency = jnp.exp(-math.log(rope_base) * exponent)
    angles = (row + length).astype(jnp.float32) * frequency
    sine = jnp.sin(angles)
    cos_s[...] = jnp.cos(angles)
    sin_s[...] = jnp.where(lane < HD // 2, -sine, sine)

    for copy in own:
        copy.wait()
    pl.semaphore_wait(barrier, 8)

    def send_tokens(slot, target):
        pltpu.make_async_remote_copy(
            src_ref=buf_t.at[slot], dst_ref=buf_t.at[slot], send_sem=t_send,
            recv_sem=t_recv.at[slot], device_id={"head": target}, device_id_type=MESH,
        ).start()

    def tokens_arrived(slot):
        pltpu.make_async_copy(buf_t.at[slot], buf_t.at[slot], t_recv.at[slot]).wait()

    streams = {
        "q": (buf_q, q_recv, w_send.at[0], MODE_Q),
        "kv": (buf_kv, kv_recv, w_send.at[1], MODE_KV),
        "o": (buf_o, o_recv, w_send.at[2], MODE_O),
    }

    def send(name, slot, target):
        buf, recv, sem, _ = streams[name]
        pltpu.make_async_remote_copy(
            src_ref=buf.at[slot], dst_ref=buf.at[slot], send_sem=sem,
            recv_sem=recv.at[slot], device_id={"tok": target}, device_id_type=MESH,
        ).start()

    def arrived(name, slot):
        buf, recv, _, _ = streams[name]
        pltpu.make_async_copy(buf.at[slot], buf.at[slot], recv.at[slot]).wait()

    def send_cache(peer):
        pltpu.make_async_remote_copy(
            src_ref=buf_in.at[peer], dst_ref=buf_c.at[me_t], send_sem=c_send,
            recv_sem=c_recv, device_id={"tok": peer}, device_id_type=MESH,
        ).start()

    half = NZ // 2

    def at_step(y, step, c):
        if step == 0:
            return [tok_id(y, z, c)]
        slots = [tok_id(y, z - step, c)]
        return slots + [tok_id(y, z + step, c)] if step < half else slots

    def start_stream(name):
        send(name, me_t, across)
        send(name, me_t, right)
        send(name, me_t, left)
        send(name, me_t, twin)

    def second_start(name):
        if streams[name][3] == "zy":
            return
        arrived(name, across)
        send(name, across, right)
        send(name, across, left)
        send(name, across, twin)

    def forward(name, step):
        rest = []
        mode = streams[name][3]
        for y in (yl,) if mode == "zy" else (yl, yl_other):
            for number, slot in enumerate(at_step(y, step, core)):
                arrived(name, slot)
                if step < half - number:
                    send(name, slot, left if number else right)
                if mode == "zy":
                    rest.append((name, slot, across))
                rest.append((name, slot, twin))
        return rest

    def across_arrivals(name, step):
        for slot in at_step(yl_other, step, core):
            if streams[name][3] == "zy":
                arrived(name, slot)
                send(name, slot, twin)
            if name == "q":
                send_cache(slot)

    def twin_arrivals(y, step):
        for slot in at_step(y, step, 1 - core):
            arrived("q", slot)
            send_cache(slot)

    start_stream("q")
    start_stream("kv")
    send_tokens(me_h, far_head)
    for i in (1, 3, 2):
        send_tokens(me_h, head_id(y_hi, i))
    second_start("q")
    second_start("kv")

    @pl.loop(0, page_ref.shape[1])
    def _(slot):
        page = jnp.int32(0)
        for p in range(page_ref.shape[1]):
            page = jnp.where(page_ref[0, p] == slot, jnp.int32(p), page)
        inv_s[slot] = page

    def square_sum():
        for slot in [head_id(y_hi, i) for i in (1, 2, 3)] + [head_id(y_far, i) for i in (1, 2, 3)]:
            tokens_arrived(slot)
        total = jnp.zeros((rows, 1), jnp.float32)
        for h in range(n_head):
            part = buf_t[h].astype(jnp.float32)
            total += jnp.sum(part * part, axis=1, keepdims=True)
        return lax.rsqrt(total / (n_head * width) + norm_eps)

    def normalise(scale):
        for h in range(n_head):
            gain = gain_ref[pl.ds(h * width, width)].astype(jnp.float32)[None, :]
            normed[h] = (buf_t[h].astype(jnp.float32) * scale * gain).astype(jnp.bfloat16)

    group = n_tok // n_head
    depth = buf_q.shape[1]

    def project():
        for y in range(2):
            for zz in range(NZ):
                arrived("kv", tok_id(y, zz, 1 - core))
        q_sum = jnp.zeros(q_s.shape, jnp.float32)
        kv_sum = jnp.zeros(kv_s.shape, jnp.float32)
        for h in range(n_head):
            lhs = normed[h]
            wq = buf_q[pl.ds(h * group, group)].reshape(group * depth, buf_q.shape[2])
            wkv = buf_kv[pl.ds(h * group, group)].reshape(group * depth, buf_kv.shape[2])
            q_sum += jnp.dot(lhs, wq, preferred_element_type=jnp.float32)
            kv_sum += jnp.dot(lhs, wkv, preferred_element_type=jnp.float32)

        def rope(v):
            return (v * cos_s[...] + pltpu.roll(v, HD // 2, 1) * sin_s[...]).astype(jnp.bfloat16)

        for head in range(q_s.shape[1] // HD):
            q_s[:, head * HD:(head + 1) * HD] = rope(q_sum[:, head * HD:(head + 1) * HD])
        kv_s[:, :HD] = rope(kv_sum[:, :HD])
        kv_s[:, HD:] = kv_sum[:, HD:].astype(jnp.bfloat16)

    def page_caches():
        pltpu.make_async_copy(
            buf_c.at[pl.ds(0, n_tok - 1)], buf_c.at[pl.ds(0, n_tok - 1)], c_recv
        ).wait()
        for number, (live, out) in enumerate(((live_k, dk_ref), (live_v, dv_ref))):
            entries = buf_c[:, number].astype(jnp.float32)
            slots, head_size = entries.shape[0] * entries.shape[1], entries.shape[2]
            entries = entries.reshape(slots, head_size)
            slot_ids = lax.broadcasted_iota(jnp.int32, (slots, head_size), 0)
            entries = jnp.where(slot_ids < length, entries, 0.0)
            live[...] = entries.reshape(live.shape).astype(jnp.bfloat16)
            for page in range(out.shape[0]):
                out[page] = live[inv_s[page]]

    def attend(head):
        columns = slice(head * HD, (head + 1) * HD)
        keys = live_k[...].reshape(n_tok * buf_c.shape[2], HD)
        values = live_v[...].reshape(n_tok * buf_c.shape[2], HD)
        score_scale = 1.0 / math.sqrt(HD)
        cached_ids = lax.broadcasted_iota(jnp.int32, (rows, keys.shape[0]), 1)
        causal = lax.broadcasted_iota(jnp.int32, (rows, rows), 1) <= lax.broadcasted_iota(
            jnp.int32, (rows, rows), 0
        )
        query = q_s[:, columns]
        cached = lax.dot_general(query, keys, NT, preferred_element_type=jnp.float32) * score_scale
        span = lax.dot_general(query, kv_s[:, :HD], NT, preferred_element_type=jnp.float32) * score_scale
        cached = jnp.where(cached_ids < length, cached, -jnp.inf)
        span = jnp.where(causal, span, -jnp.inf)
        top = jnp.maximum(
            jnp.max(cached, axis=1, keepdims=True), jnp.max(span, axis=1, keepdims=True)
        )
        cached = jnp.exp(cached - top)
        span = jnp.exp(span - top)
        whole = jnp.sum(cached, axis=1, keepdims=True) + jnp.sum(span, axis=1, keepdims=True)
        out = jnp.dot((cached / whole).astype(jnp.bfloat16), values, preferred_element_type=jnp.float32)
        out += jnp.dot((span / whole).astype(jnp.bfloat16), kv_s[:, HD:], preferred_element_type=jnp.float32)
        att_s[:, columns] = out.astype(jnp.bfloat16)

    heads = q_s.shape[1] // HD
    waiting = []
    for step in range(half + 1):
        waiting.append((min(step + GAP, half + 1), functools.partial(across_arrivals, "q", step)))
    for step in range(half + 1):
        waiting.append((min(step + GAP, half + 1), functools.partial(twin_arrivals, yl, step)))
        waiting.append((min(step + 2 * GAP, half + 1), functools.partial(twin_arrivals, yl_other, step)))
        waiting.append((LAG + step + GAP, functools.partial(across_arrivals, "o", step)))
    if LAG == 0:
        start_stream("o")
    for step in range(1, half + LAST + 1):
        rest = []
        if step <= half:
            rest += forward("q", step)
            rest += forward("kv", step)
        if step == LAG + 1:
            second_start("o")
        if LAG < step <= half + LAG:
            rest += forward("o", step - LAG)
        if step == LAG:
            start_stream("o")
        for name, slot, target in rest:
            send(name, slot, target)
        for due, action in waiting:
            if due == step:
                action()
        if step <= half:
            for slot in at_step(yl, step, core):
                send_cache(slot)
        if step == 1:
            tokens_arrived(far_head)
            for i in (1, 3, 2):
                send_tokens(far_head, head_id(y_hi, i))
        if step == half - 1:
            normalise(square_sum())
        if step == half + 1:
            project()
        if step == half + 2:
            page_caches()
            attend(0)
        if step == half + 3:
            for head in range(1, heads):
                attend(head)
    for due, action in waiting:
        if due > half + LAST:
            action()
    for y in range(2):
        for zz in range(NZ):
            arrived("o", tok_id(y, zz, 1 - core))

    def partial_block(g):
        block = buf_o[pl.ds(g * group, group)].reshape(group * depth, buf_o.shape[2])
        return lax.dot_general(att_s[...], block, NT, preferred_element_type=jnp.float32)

    def part_copy(slot, target):
        return pltpu.make_async_remote_copy(
            src_ref=part_send.at[slot], dst_ref=part_recv.at[slot], send_sem=p_send.at[slot],
            recv_sem=p_recv.at[slot], device_id={"head": target}, device_id_type=MESH,
        )

    copies = [part_copy(i - 1, head_id(y_hi, i)) for i in (1, 2, 3)]
    copies += [part_copy(i + 2, head_id(y_hi, i)) for i in (1, 2, 3)]
    copies += [part_copy(6, far_head)]
    for i in (2, 1, 3):
        part_send[i - 1] = partial_block(head_id(y_far, i)).astype(jnp.bfloat16)
        copies[i - 1].start()
    far_sum = partial_block(far_head)
    for i in (2, 1, 3):
        part_send[i + 2] = partial_block(head_id(y_hi, i)).astype(jnp.bfloat16)
        copies[i + 2].start()
    for i in (1, 3, 2):
        copies[i - 1].wait_recv()
        far_sum += part_recv[i - 1].astype(jnp.float32)
    part_send[6] = far_sum.astype(jnp.bfloat16)
    copies[6].start()
    mixed = partial_block(me_h)
    for i in (1, 3, 2):
        copies[i + 2].wait_recv()
        mixed += part_recv[i + 2].astype(jnp.float32)
    copies[6].wait_recv()
    mixed_ref[...] = (mixed + part_recv[6].astype(jnp.float32)).astype(mixed_ref.dtype)

    for copy in copies:
        copy.wait_send()
    pltpu.make_async_copy(
        buf_t.at[pl.ds(0, n_head - 1)], buf_t.at[pl.ds(0, n_head - 1)], t_send
    ).wait()
    pltpu.make_async_copy(
        buf_c.at[pl.ds(0, n_tok - 1)], buf_c.at[pl.ds(0, n_tok - 1)], c_send
    ).wait()
    for buf, _, sem, _ in streams.values():
        pltpu.make_async_copy(
            buf.at[pl.ds(0, n_tok - 1)], buf.at[pl.ds(0, n_tok - 1)], sem
        ).wait()


def solution(mesh):
    n_tok, n_head = mesh.shape["tok"], mesh.shape["head"]

    def shards(tokens, gain, w_query, w_key, w_value, w_out, cache_keys, cache_values, lengths, page_table):
        rows, width = tokens.shape
        pages = page_table.shape[1]
        depth, head_cols = w_query.shape
        page_size = n_tok * cache_keys.shape[1] // pages
        paged = (pages, page_size, cache_keys.shape[2])
        bf16 = jnp.bfloat16
        dma = pltpu.SemaphoreType.DMA
        hbm = pl.BlockSpec(memory_space=pl.ANY)
        vmem = pl.BlockSpec(memory_space=pltpu.VMEM)
        smem = pl.BlockSpec(memory_space=pltpu.SMEM)
        return pl.pallas_call(
            functools.partial(kernel, n_tok, n_head),
            out_shape=(
                jax.ShapeDtypeStruct((rows, width), bf16),
                jax.ShapeDtypeStruct(paged, bf16),
                jax.ShapeDtypeStruct(paged, bf16),
            ),
            in_specs=[smem, smem, vmem] + [hbm] * 7,
            out_specs=(vmem, vmem, vmem),
            scratch_shapes=[
                pltpu.VMEM((n_head, rows, width), bf16),
                pltpu.VMEM((n_tok, depth, head_cols), bf16),
                pltpu.VMEM((n_tok, depth, 2 * HD), bf16),
                pltpu.VMEM((n_tok, depth, head_cols), bf16),
                pltpu.VMEM((n_tok, 2) + cache_keys.shape[1:], bf16),
                pltpu.VMEM((n_tok, 2) + cache_keys.shape[1:], bf16),
                pltpu.VMEM((n_head, rows, width), bf16),
                pltpu.VMEM(paged, bf16),
                pltpu.VMEM(paged, bf16),
                pltpu.VMEM((n_head - 1, rows, width), bf16),
                pltpu.VMEM((n_head - 1, rows, width), bf16),
                pltpu.VMEM((rows, head_cols), bf16),
                pltpu.VMEM((rows, 2 * HD), bf16),
                pltpu.VMEM((rows, HD), jnp.float32),
                pltpu.VMEM((rows, HD), jnp.float32),
                pltpu.VMEM((rows, head_cols), bf16),
                pltpu.SMEM((pages,), jnp.int32),
                dma((9,)),
                dma((n_head,)),
                dma((n_tok,)),
                dma((n_tok,)),
                dma((n_tok,)),
                dma,
                dma((n_head - 1,)),
                dma,
                dma((3,)),
                dma,
                dma((n_head - 1,)),
            ],
            compiler_params=pltpu.CompilerParams(collective_id=0, has_side_effects=True),
        )(lengths, page_table, gain, tokens, w_query, w_key, w_value, w_out, cache_keys, cache_values)

    in_specs = (
        P("tok", "head"), P(), P("tok", "head"), P("tok", "head"), P("tok", "head"),
        P("tok", "head"), P(None, "tok", "head"), P(None, "tok", "head"), P("tok"), P("tok", None),
    )
    out_specs = (P("tok", "head"), P("tok", None, "head"), P("tok", None, "head"))
    return jax.shard_map(shards, mesh=mesh, in_specs=in_specs, out_specs=out_specs, check_vma=False)
```
